32 devices in a mesh: groups: 2 (over y), chan: 8 (over z, x), tm: 2 (over core).
Axes of the slice: x: 2, y: 2, z: 4, core: 2. Of those that a mesh axis runs over, the one named last changes fastest.
Arguments:
- record: bfloat16 [8, 4096, 1000], P('tm', ('groups', 'chan')), parts along dimension 1
- flags: int32 [4096], P(('groups', 'chan')), parts along dimension 0, may hold values 0 or 1
- plan: int32 [4], replicated, may hold values from 1 to 7, as said below
Outputs:
- stacked: bfloat16 [4, 4, 4096, 256], P('tm', None, ('groups', 'chan')), parts along dimension 2
The draws below stay inside these ranges and needn't reach their ends.
There are 2 independent parts, one for each index of `groups`. The reference program is written for one: setup_inputs(seed, part) draws one part's arguments, and reference() takes and returns one part's arrays. A program takes and returns all parts, laid end to end along the dimension named above; an argument that names none is the same for every part. Nothing has to cross between parts.
Inputs may be any that keep to these rules, and one draw needn't show every extreme that they name: `plan`: 4 distinct offsets; one of them equals 7.
All inputs are finite; a program needn't handle non-finite values. No bound on the sum of `flags` on one device may be relied on, other than what follows from the above.
Results may differ from the reference program's by a relative error of at most 0.0082.
Values may be sent and summed in bfloat16 or wider, within the bound.
No kernel may reach another device: no remote copies, remote signals or barrier semaphores. Data moves between devices by JAX's collectives and lax.ppermute only.
A program may use at most 64 MiB of HBM per device.

```python
import math
import jax
import jax.numpy as jnp
from jax import lax

CH_DEV = 256
SAMPLES = 1000
NFREQ = 32
FLO = 5
LAGS = 4
LAGSTEP = 3
ROUNDS = 4
CHANNELS = 2048
WINDOWS = 8
N_CHAN = 8


def draw_record(key, part):
    scale_key, noise_key = jax.random.split(key, 2)
    shape = (WINDOWS, CHANNELS, SAMPLES)
    scales = jnp.exp(jax.random.uniform(scale_key, (WINDOWS, CHANNELS, 1), jnp.float32) * math.log(10.0))
    values = scales * jax.random.normal(noise_key, shape, jnp.float32)
    return values.astype(jnp.bfloat16)


def draw_plan(key, part):
    first_key, second_key = jax.random.split(key)
    others = jax.random.permutation(first_key, N_CHAN - 2)[:ROUNDS - 1] + 1
    values = jnp.concatenate([others.astype(jnp.int32), jnp.full((1,), N_CHAN - 1, jnp.int32)])
    order = jax.random.permutation(second_key, ROUNDS)
    return values[order].astype(jnp.int32)


def with_ends(result, rng, smallest, largest):
    extent = result.shape
    index_at = [jax.random.randint(jax.random.fold_in(rng, axis), (), 0, extent[axis]) for axis in range(len(extent))]
    result = result.at[tuple(index_at)].set(smallest)
    longest = extent.index(max(extent))
    index_at[longest] = (index_at[longest] + 1) % extent[longest]
    return result.at[tuple(index_at)].set(largest)


def setup_inputs(seed: int = 0, part: int = 0) -> dict:
    key_of = jax.random.split(jax.random.key(seed), 4)
    part_keys = jax.random.split(jax.random.fold_in(key_of[3], part), 4)
    return {
        "record": draw_record(jax.random.fold_in(jax.random.fold_in(key_of[3], part), 71), part),
        "flags": with_ends((jax.random.randint(part_keys[1], (CHANNELS,), 0, 8) < 7).astype(jnp.int32), jax.random.fold_in(part_keys[1], 1), 0, 1),
        "plan": draw_plan(jax.random.fold_in(key_of[3], 71), part),
    }


TWO_PI = 2.0 * math.pi

def prepare_traces(trace, flags):
    values = trace.astype(jnp.float32)
    centred = values - lax.optimization_barrier(jnp.mean(values, axis=-1, keepdims=True))
    spread = jnp.sqrt(lax.optimization_barrier(jnp.mean(centred * centred, axis=-1, keepdims=True)) + 1e-05)
    return (centred / spread * flags.astype(jnp.float32)[:, None]).astype(jnp.bfloat16)

def make_basis():
    times = jnp.arange(SAMPLES, dtype=jnp.int32)
    bins = FLO + jnp.arange(NFREQ, dtype=jnp.int32)
    phase = bins[:, None] * times[None, :] % SAMPLES
    angle = phase.astype(jnp.float32) * (TWO_PI / SAMPLES)
    table = jnp.stack([jnp.cos(angle), -jnp.sin(angle)], axis=1)
    return table.reshape(2 * NFREQ, SAMPLES).astype(jnp.bfloat16)

def lag_angles(first_bin, count_bins, lag_start, count_lags):
    lag_ticks = (lag_start + jnp.arange(count_lags, dtype=jnp.int32) - LAGS // 2) * LAGSTEP
    bins = FLO + first_bin + jnp.arange(count_bins, dtype=jnp.int32)
    phase = bins[None, :] * lag_ticks[:, None] % SAMPLES
    return phase.astype(jnp.float32) * (TWO_PI / SAMPLES)

def rotate_spectra(spectra, angles):
    real_part = spectra[:, :, 0, :].astype(jnp.float32)[None]
    imag_part = spectra[:, :, 1, :].astype(jnp.float32)[None]
    cosine = jnp.cos(angles)[:, None, :, None]
    sine = jnp.sin(angles)[:, None, :, None]
    first = real_part * cosine + imag_part * sine
    second = imag_part * cosine - real_part * sine
    return jnp.stack([first, second], axis=3).astype(jnp.bfloat16)

def reference(record, flags, plan):
    basis = make_basis()
    inverse = 1.0 / math.sqrt(SAMPLES)

    def one_window(trace):
        scaled = prepare_traces(trace, flags)
        return (jnp.dot(basis, scaled.T, preferred_element_type=jnp.float32) * inverse).astype(jnp.bfloat16)
    spectra = lax.map(one_window, record).reshape(WINDOWS, NFREQ, 2, CHANNELS)
    angles = lag_angles(0, NFREQ, 0, LAGS)
    scale_out = 1.0 / math.sqrt(WINDOWS * NFREQ)

    def one_block(block):
        own = lax.dynamic_slice_in_dim(spectra, block * CH_DEV, CH_DEV, 3)
        turned = rotate_spectra(own, angles).astype(jnp.float32)
        results = []
        for round_index in range(ROUNDS):
            other = jnp.bitwise_xor(block, plan[round_index]).astype(jnp.int32)
            partner = lax.dynamic_slice_in_dim(spectra, other * CH_DEV, CH_DEV, 3).astype(jnp.float32)
            piece = jnp.einsum('lwfpa,wfpb->lab', turned, partner) * scale_out
            results.append(piece.astype(jnp.bfloat16))
        return jnp.stack(results, axis=1)
    blocks = lax.map(one_block, jnp.arange(N_CHAN, dtype=jnp.int32))
    return blocks.transpose(1, 2, 0, 3, 4).reshape(LAGS, ROUNDS, CHANNELS, CH_DEV)
```

```python
from functools import partial
import itertools
import math

import numpy as np

import jax
import jax.numpy as jnp
from jax import lax
from jax.experimental import pallas as pl
from jax.experimental.pallas import tpu as pltpu
from jax.sharding import PartitionSpec as P

NFREQ = 32
FLO = 5
LAGS = 4
LAGSTEP = 3
ROUNDS = 4

TWO_PI = 2.0 * math.pi
VMEM = pltpu.MemorySpace.VMEM
SMEM = pltpu.MemorySpace.SMEM
BF16 = jnp.bfloat16
F32 = jnp.float32


def padded(samples):
    return -(-samples // 256) * 256


def basis_table(samples):
    phase = (FLO + np.arange(NFREQ))[:, None] * np.arange(samples)[None, :] % samples
    angle = phase.astype(np.float32) * np.float32(TWO_PI / samples)
    rows = np.concatenate([np.cos(angle), -np.sin(angle)], 0).astype(jnp.bfloat16)
    table = np.zeros((2 * NFREQ + 16, padded(samples)), jnp.bfloat16)
    table[: 2 * NFREQ, :samples] = rows
    table[2 * NFREQ, :samples] = 1
    sums = rows.astype(np.float64).sum(1).astype(np.float32)
    return table, np.repeat(sums[:, None], 128, 1)


def turn_table(samples):
    ticks = (np.arange(LAGS) - LAGS // 2) * LAGSTEP
    phase = (FLO + np.arange(NFREQ))[None, :] * ticks[:, None] % samples
    angle = phase.astype(np.float32) * np.float32(TWO_PI / samples)
    table = np.stack([np.cos(angle), np.sin(angle)], 1).astype(np.float32)
    return np.repeat(table[..., None], 128, 3)


def offset_sets(n_chan):
    others = itertools.combinations(range(1, n_chan - 1), ROUNDS - 1)
    return sorted(others, key=lambda s: s[::-1])


def set_index(n_chan, plan):
    ranks = []
    index = jnp.int32(0)
    for r in range(ROUNDS):
        rank = jnp.int32(0)
        for j in range(ROUNDS):
            if j != r:
                rank += (plan[j] < plan[r]).astype(jnp.int32)
        ranks.append(rank)
        below = plan[r] - 1
        choose = [below, below * (below - 1) // 2, below * (below - 1) * (below - 2) // 6]
        term = jnp.where(rank == 0, choose[0], jnp.where(rank == 1, choose[1], choose[2]))
        index += jnp.where(rank == ROUNDS - 1, 0, term)
    return index, ranks


def spectra_kernel(n_chan, plan_ref, flags_ref, basis_ref, sums_ref, record_ref, spec_ref, index_ref, held, sems):
    windows, samples, width = record_ref.shape
    copies = [
        pltpu.make_async_copy(record_ref.at[w], held.at[w, pl.ds(0, samples)], sems.at[w])
        for w in range(windows)
    ]
    for copy in copies:
        copy.start()
    index, _ = set_index(n_chan, [plan_ref[r] for r in range(ROUNDS)])
    index_ref[0] = index
    pad = held.shape[1] - samples
    for w in range(windows):
        held[w, samples:, :] = jnp.zeros((pad, width), BF16)
    good = flags_ref[...].astype(F32) * (1.0 / math.sqrt(samples))
    sums = jnp.concatenate([sums_ref[...]] * (width // 128), axis=1)
    rows = 2 * NFREQ
    for w in range(windows):
        copies[w].wait()
        out = jnp.dot(basis_ref[...], held[w], preferred_element_type=F32)
        mean = out[rows : rows + 1] * (1.0 / samples)
        centred = held[w, :samples, :].astype(F32) - mean
        power = jnp.sum(centred * centred, axis=0, keepdims=True) * (1.0 / samples)
        scale = good / jnp.sqrt(power + 1e-05)
        spec_ref[w * rows : (w + 1) * rows, :] = ((out[:rows] - sums * mean) * scale).astype(BF16)


def turn_kernel(mine_ref, other_ref, table_ref, turned_ref):
    lags = turned_ref.shape[0]
    first = lax.axis_index("tm") * lags
    depth, width = mine_ref.shape
    for half, ref in enumerate((mine_ref, other_ref)):
        for lag in range(lags):
            cosine = jnp.concatenate([table_ref[first + lag, 0]] * (width // 128), axis=1)
            sine = jnp.concatenate([table_ref[first + lag, 1]] * (width // 128), axis=1)
            parts = []
            for w in range(depth // (2 * NFREQ)):
                start = w * 2 * NFREQ
                real = ref[start : start + NFREQ, :].astype(F32)
                imag = ref[start + NFREQ : start + 2 * NFREQ, :].astype(F32)
                parts += [real * cosine + imag * sine, imag * cosine - real * sine]
            turned = jnp.concatenate(parts, axis=0).T.astype(BF16)
            turned_ref[lag, :, half * depth : (half + 1) * depth] = turned


def correlate_kernel(scale, sort, plan_ref, turned_ref, *refs):
    blocks, (out_ref, held, sems) = refs[: 2 * ROUNDS], refs[2 * ROUNDS :]
    lags, width, depth = turned_ref.shape
    half = depth // 2
    plan = [plan_ref[r] for r in range(ROUNDS)]
    places = [jnp.int32(s) for s in range(ROUNDS)]
    if sort:
        places = [jnp.int32(0)] * ROUNDS
        for r in range(ROUNDS):
            rank = jnp.int32(0)
            for j in range(ROUNDS):
                if j != r:
                    rank += (plan[j] < plan[r]).astype(jnp.int32)
            for s in range(ROUNDS):
                places[s] = jnp.where(rank == s, r, places[s])
    copies = []
    for s in range(ROUNDS):
        for lag in range(lags):
            total = jnp.dot(turned_ref[lag, :, :half], blocks[s][...], preferred_element_type=F32)
            total += jnp.dot(turned_ref[lag, :, half:], blocks[ROUNDS + s][...], preferred_element_type=F32)
            held[s, lag] = (total * scale).astype(BF16)
            copy = pltpu.make_async_copy(held.at[s, lag], out_ref.at[lag, places[s]], sems.at[s, lag])
            copy.start()
            copies.append(copy)
    for copy in copies:
        copy.wait()


def hop(value, offset):
    pairs = [(source, source ^ offset) for source in range(lax.axis_size("chan"))]
    return lax.ppermute(value, "chan", pairs)


def swap(value):
    return lax.ppermute(value, "tm", [(0, 1), (1, 0)])


def fetch_set(offsets, spec):
    n_chan = lax.axis_size("chan")
    top = n_chan - 1
    far = hop(spec, top)
    got = {top: far}
    for offset in offsets:
        if offset < n_chan // 2:
            got[offset] = hop(spec, offset)
    for offset in offsets:
        if offset >= n_chan // 2:
            got[offset] = hop(far, offset ^ top)
    mine = [got[offset] for offset in sorted(got)]
    return tuple(mine) + tuple(swap(m) for m in mine)


def fetch_by_bits(spec, plan):
    bits = lax.axis_size("chan").bit_length() - 1
    partners = [spec] * ROUNDS
    for bit in range(bits):
        moves = jnp.right_shift(plan, bit) & 1 == 1
        for r in range(ROUNDS):
            partners[r] = lax.cond(moves[r], partial(hop, offset=2**bit), lambda v: v, partners[r])
    return tuple(partners) + tuple(swap(m) for m in partners)


def on_device(record, flags, plan):
    windows, width, samples = record.shape
    n_chan = lax.axis_size("chan")
    lags = LAGS // lax.axis_size("tm")
    depth = windows * 2 * NFREQ
    basis, sums = basis_table(samples)
    spec, index = pl.pallas_call(
        partial(spectra_kernel, n_chan),
        out_shape=(jax.ShapeDtypeStruct((depth, width), BF16), jax.ShapeDtypeStruct((1,), jnp.int32)),
        in_specs=[
            pl.BlockSpec(memory_space=SMEM),
            pl.BlockSpec(memory_space=VMEM),
            pl.BlockSpec(memory_space=VMEM),
            pl.BlockSpec(memory_space=VMEM),
            pl.BlockSpec(memory_space=pl.ANY),
        ],
        out_specs=(pl.BlockSpec(memory_space=VMEM), pl.BlockSpec(memory_space=SMEM)),
        scratch_shapes=[pltpu.VMEM((windows, padded(samples), width), BF16), pltpu.SemaphoreType.DMA((windows,))],
        name="spectra",
    )(plan, flags.reshape(1, width), jnp.asarray(basis), jnp.asarray(sums), record.transpose(0, 2, 1))

    sets = math.comb(n_chan - 2, ROUNDS - 1)
    if sets <= 64:
        blocks = lax.switch(index[0], [partial(fetch_set, s) for s in offset_sets(n_chan)], spec)
    else:
        blocks = fetch_by_bits(spec, plan)

    turned = pl.pallas_call(
        turn_kernel,
        out_shape=jax.ShapeDtypeStruct((lags, width, 2 * depth), BF16),
        in_specs=[pl.BlockSpec(memory_space=VMEM)] * 3,
        out_specs=pl.BlockSpec(memory_space=VMEM),
        name="turn",
    )(spec, swap(spec), jnp.asarray(turn_table(samples)))

    total_windows = windows * lax.axis_size("tm")
    return pl.pallas_call(
        partial(correlate_kernel, 1.0 / math.sqrt(total_windows * NFREQ), sets <= 64),
        out_shape=jax.ShapeDtypeStruct((lags, ROUNDS, width, width), BF16),
        in_specs=[pl.BlockSpec(memory_space=SMEM)] + [pl.BlockSpec(memory_space=VMEM)] * (1 + 2 * ROUNDS),
        out_specs=pl.BlockSpec(memory_space=pl.ANY),
        scratch_shapes=[
            pltpu.VMEM((ROUNDS, lags, width, width), BF16),
            pltpu.SemaphoreType.DMA((ROUNDS, lags)),
        ],
        name="correlate",
    )(plan, turned, *blocks)


def solution(mesh):
    return jax.shard_map(
        on_device,
        mesh=mesh,
        in_specs=(P("tm", ("groups", "chan"), None), P(("groups", "chan")), P()),
        out_specs=P("tm", None, ("groups", "chan"), None),
        check_vma=False,
    )
```

```python
from functools import partial
import math

import numpy as np

import jax
import jax.numpy as jnp
from jax import lax
from jax.experimental import pallas as pl
from jax.experimental.pallas import tpu as pltpu
from jax.sharding import PartitionSpec as P

NFREQ = 32
FLO = 5
LAGS = 4
LAGSTEP = 3
ROUNDS = 4

TWO_PI = 2.0 * math.pi
VMEM = pltpu.MemorySpace.VMEM
SMEM = pltpu.MemorySpace.SMEM
BF16 = jnp.bfloat16
F32 = jnp.float32


def padded(samples):
    return -(-samples // 256) * 256


def basis_table(samples):
    phase = (FLO + np.arange(NFREQ))[:, None] * np.arange(samples)[None, :] % samples
    angle = phase.astype(np.float32) * np.float32(TWO_PI / samples)
    rows = np.concatenate([np.cos(angle), -np.sin(angle)], 0).astype(jnp.bfloat16)
    table = np.zeros((2 * NFREQ + 16, padded(samples)), jnp.bfloat16)
    table[: 2 * NFREQ, :samples] = rows
    table[2 * NFREQ, :samples] = 1
    sums = rows.astype(np.float64).sum(1).astype(np.float32)
    return table, np.repeat(sums[:, None], 128, 1)


def turn_table(samples):
    ticks = (np.arange(LAGS) - LAGS // 2) * LAGSTEP
    phase = (FLO + np.arange(NFREQ))[None, :] * ticks[:, None] % samples
    angle = phase.astype(np.float32) * np.float32(TWO_PI / samples)
    table = np.stack([np.cos(angle), np.sin(angle)], 1).astype(np.float32)
    return np.repeat(table[..., None], 128, 3)


def ranks_of(plan):
    ranks = []
    for r in range(ROUNDS):
        ranks.append(sum((plan[j] < plan[r]).astype(jnp.int32) for j in range(ROUNDS) if j != r))
    return ranks


def round_of(rank, ranks):
    found = jnp.int32(0)
    for r in range(ROUNDS):
        found = jnp.where(ranks[r] == rank, r, found)
    return found


def hop_masks(n_chan, plan):
    near, far = jnp.int32(0), jnp.int32(0)
    for d in range(1, n_chan // 2):
        for r in range(ROUNDS):
            near += (plan[r] == d).astype(jnp.int32) << (d - 1)
            far += (plan[r] == d ^ (n_chan - 1)).astype(jnp.int32) << (d - 1)
    return near, far


def spectra_kernel(n_chan, plan_ref, flags_ref, basis_ref, sums_ref, record_ref, spec_ref, near_ref, far_ref, held, sems):
    windows, samples, width = record_ref.shape
    copies = [
        pltpu.make_async_copy(record_ref.at[w], held.at[w, pl.ds(0, samples)], sems.at[w])
        for w in range(windows)
    ]
    for copy in copies:
        copy.start()
    if few_sets(n_chan):
        near_ref[0], far_ref[0] = hop_masks(n_chan, [plan_ref[r] for r in range(ROUNDS)])
    else:
        near_ref[0] = far_ref[0] = jnp.int32(0)
    pad = held.shape[1] - samples
    for w in range(windows):
        held[w, samples:, :] = jnp.zeros((pad, width), BF16)
    good = flags_ref[...].astype(F32) * (1.0 / math.sqrt(samples))
    sums = jnp.concatenate([sums_ref[...]] * (width // 128), axis=1)
    rows = 2 * NFREQ
    for w in range(windows):
        copies[w].wait()
        out = jnp.dot(basis_ref[...], held[w], preferred_element_type=F32)
        mean = out[rows : rows + 1] * (1.0 / samples)
        centred = held[w, :samples, :].astype(F32) - mean
        power = jnp.sum(centred * centred, axis=0, keepdims=True) * (1.0 / samples)
        scale = good / jnp.sqrt(power + 1e-05)
        spec_ref[w * rows : (w + 1) * rows, :] = ((out[:rows] - sums * mean) * scale).astype(BF16)


def turn_kernel(mine_ref, other_ref, table_ref, turned_ref):
    lags = turned_ref.shape[0]
    first = lax.axis_index("tm") * lags
    depth, width = mine_ref.shape
    for half, ref in enumerate((mine_ref, other_ref)):
        for lag in range(lags):
            cosine = jnp.concatenate([table_ref[first + lag, 0]] * (width // 128), axis=1)
            sine = jnp.concatenate([table_ref[first + lag, 1]] * (width // 128), axis=1)
            parts = []
            for w in range(depth // (2 * NFREQ)):
                start = w * 2 * NFREQ
                real = ref[start : start + NFREQ, :].astype(F32)
                imag = ref[start + NFREQ : start + 2 * NFREQ, :].astype(F32)
                parts += [real * cosine + imag * sine, imag * cosine - real * sine]
            turned = jnp.concatenate(parts, axis=0).T.astype(BF16)
            turned_ref[lag, :, half * depth : (half + 1) * depth] = turned


def correlate_kernel(scale, ranks, plan_ref, turned_ref, *refs):
    blocks = len(ranks)
    mine, other, (out_ref, held, sems) = refs[:blocks], refs[blocks : 2 * blocks], refs[-3:]
    lags, width, depth = turned_ref.shape
    half = depth // 2
    plan_ranks = ranks_of([plan_ref[r] for r in range(ROUNDS)])
    copies = []
    for s, rank in enumerate(ranks):
        if isinstance(rank, tuple):
            rank = jnp.where(lax.axis_index("tm") == 0, *rank)
        place = s if rank is None else round_of(rank, plan_ranks)
        for lag in range(lags):
            total = jnp.dot(turned_ref[lag, :, :half], mine[s][...], preferred_element_type=F32)
            total += jnp.dot(turned_ref[lag, :, half:], other[s][...], preferred_element_type=F32)
            held[s, lag] = (total * scale).astype(BF16)
            copies.append(pltpu.make_async_copy(held.at[s, lag], out_ref.at[lag, place], sems.at[s, lag]))
            copies[-1].start()
    for copy in copies:
        copy.wait()


def correlate(plan, turned, pairs, ranks, out=None):
    lags, width, depth = turned.shape
    blocks = len(pairs)
    scale = 1.0 / math.sqrt(depth // 2)
    given = [plan, turned] + [p[0] for p in pairs] + [p[1] for p in pairs]
    specs = [pl.BlockSpec(memory_space=SMEM)] + [pl.BlockSpec(memory_space=VMEM)] * (1 + 2 * blocks)
    if out is not None:
        given.append(out)
        specs.append(pl.BlockSpec(memory_space=pl.ANY))
    return pl.pallas_call(
        partial(correlate_kernel, scale, ranks),
        out_shape=jax.ShapeDtypeStruct((lags, ROUNDS, width, width), BF16),
        in_specs=specs,
        out_specs=pl.BlockSpec(memory_space=pl.ANY),
        scratch_shapes=[
            pltpu.VMEM((blocks, lags, width, width), BF16),
            pltpu.SemaphoreType.DMA((blocks, lags)),
        ],
        input_output_aliases={} if out is None else {len(given) - 1: 0},
        compiler_params=pltpu.CompilerParams(vmem_limit_bytes=KERNEL_VMEM),
        cost_estimate=pl.CostEstimate(flops=blocks << 28, bytes_accessed=blocks << 20, transcendentals=0),
        name="correlate",
    )(*given)


def turn(spec, samples):
    depth, width = spec.shape
    return pl.pallas_call(
        turn_kernel,
        out_shape=jax.ShapeDtypeStruct((LAGS // 2, width, 2 * depth), BF16),
        in_specs=[pl.BlockSpec(memory_space=VMEM)] * 3,
        out_specs=pl.BlockSpec(memory_space=VMEM),
        compiler_params=pltpu.CompilerParams(vmem_limit_bytes=KERNEL_VMEM),
        cost_estimate=pl.CostEstimate(flops=4 << 20, bytes_accessed=4 << 20, transcendentals=0),
        name="turn",
    )(spec, swap(spec), jnp.asarray(turn_table(samples)))


KERNEL_VMEM = 8 << 20


def few_sets(n_chan):
    return n_chan <= 2 * ROUNDS


def hop(value, offset):
    pairs = [(source, source ^ offset) for source in range(lax.axis_size("chan"))]
    return lax.ppermute(value, "chan", pairs)


def swap(value):
    return lax.ppermute(value, "tm", [(0, 1), (1, 0)])


def with_swap(block):
    return block, swap(block)


def wanted_hops(mask):
    return [d + 1 for d in range(mask.bit_length()) if mask >> d & 1]


def fetch_near(mask, spec):
    got = [with_swap(hop(spec, d)) for d in wanted_hops(mask)]
    got += [(spec, spec)] * (ROUNDS - 1 - len(got))
    return tuple(got[: ROUNDS - 1])


def correlate_mask(mask, far, near, turned, plan):
    n_chan = lax.axis_size("chan")
    hops = wanted_hops(mask)[::-1]
    first_rank = ROUNDS - 1 - len(hops)
    first, first_ranks = list(near[:first_rank]), list(range(first_rank))
    last, last_ranks = [with_swap(far)], [ROUNDS - 1]
    if hops:
        first, first_ranks = first + last, first_ranks + last_ranks
        last_ranks = [first_rank + i for i in range(len(hops))]
        if len(hops) == 2:
            got = []
            for low, high in (hops, hops[::-1]):
                pairs = [(2 * c + t, 2 * (c ^ (high if t else low)) + t) for c in range(n_chan) for t in range(2)]
                got.append(lax.ppermute(far, ("chan", "tm"), pairs))
            last = [(got[0], swap(got[1])), (got[1], swap(got[0]))]
            last_ranks = [tuple(last_ranks), tuple(last_ranks[::-1])]
        else:
            last = [with_swap(hop(far, d)) for d in hops]
    out = correlate(plan, turned, first, first_ranks)
    return correlate(plan, turned, last, last_ranks, out)


def fetch_by_bits(spec, plan):
    bits = lax.axis_size("chan").bit_length() - 1
    partners = [spec] * ROUNDS
    for bit in range(bits):
        moves = jnp.right_shift(plan, bit) & 1 == 1
        for r in range(ROUNDS):
            partners[r] = lax.cond(moves[r], partial(hop, offset=2**bit), lambda v: v, partners[r])
    return partners


def on_device(record, flags, plan):
    windows, width, samples = record.shape
    n_chan = lax.axis_size("chan")
    depth = windows * 2 * NFREQ
    basis, sums = basis_table(samples)
    mask = jax.ShapeDtypeStruct((1,), jnp.int32)
    spec, near, far = pl.pallas_call(
        partial(spectra_kernel, n_chan),
        out_shape=(jax.ShapeDtypeStruct((depth, width), BF16), mask, mask),
        in_specs=[
            pl.BlockSpec(memory_space=SMEM),
            pl.BlockSpec(memory_space=VMEM),
            pl.BlockSpec(memory_space=VMEM),
            pl.BlockSpec(memory_space=VMEM),
            pl.BlockSpec(memory_space=pl.ANY),
        ],
        out_specs=(pl.BlockSpec(memory_space=VMEM),) + (pl.BlockSpec(memory_space=SMEM),) * 2,
        scratch_shapes=[pltpu.VMEM((windows, padded(samples), width), BF16), pltpu.SemaphoreType.DMA((windows,))],
        name="spectra",
    )(plan, flags.reshape(1, width), jnp.asarray(basis), jnp.asarray(sums), record.transpose(0, 2, 1))

    if few_sets(n_chan):
        masks = range(2 ** (n_chan // 2 - 1))
        crossed = hop(spec, n_chan - 1)
        turned = turn(spec, samples)
        blocks = lax.switch(near[0], [partial(fetch_near, m) for m in masks], spec)
        return lax.switch(far[0], [partial(correlate_mask, m) for m in masks], crossed, blocks, turned, plan)
    pairs = [with_swap(m) for m in fetch_by_bits(spec, plan)]
    return correlate(plan, turn(spec, samples), pairs, [None] * ROUNDS)


def solution(mesh):
    return jax.shard_map(
        on_device,
        mesh=mesh,
        in_specs=(P("tm", ("groups", "chan"), None), P(("groups", "chan")), P()),
        out_specs=P("tm", None, ("groups", "chan"), None),
        check_vma=False,
    )
```

```python
from functools import partial
import math

import numpy as np

import jax
import jax.numpy as jnp
from jax import lax
from jax.experimental import pallas as pl
from jax.experimental.pallas import tpu as pltpu
from jax.sharding import PartitionSpec as P


NFREQ = 32
FLO = 5
LAGS = 4
LAGSTEP = 3
ROUNDS = 4

TWO_PI = 2.0 * math.pi
VMEM = pltpu.MemorySpace.VMEM
SMEM = pltpu.MemorySpace.SMEM
HBM = pltpu.MemorySpace.HBM
BF16 = jnp.bfloat16
F32 = jnp.float32


def padded(samples):
    return -(-samples // 256) * 256


def basis_table(samples):
    phase = (FLO + np.arange(NFREQ))[:, None] * np.arange(samples)[None, :] % samples
    angle = phase.astype(np.float32) * np.float32(TWO_PI / samples)
    rows = np.concatenate([np.cos(angle), -np.sin(angle)], 0).astype(jnp.bfloat16)
    table = np.zeros((2 * NFREQ + 16, padded(samples)), jnp.bfloat16)
    table[: 2 * NFREQ, :samples] = rows
    table[2 * NFREQ, :samples] = 1
    sums = rows.astype(np.float64).sum(1).astype(np.float32)
    return table, np.repeat(sums[:, None], 128, 1)


def turn_table(samples):
    ticks = (np.arange(LAGS) - LAGS // 2) * LAGSTEP
    phase = (FLO + np.arange(NFREQ))[None, :] * ticks[:, None] % samples
    angle = phase.astype(np.float32) * np.float32(TWO_PI / samples)
    table = np.stack([np.cos(angle), np.sin(angle)], 1).astype(np.float32)
    return np.repeat(table[..., None], 128, 3)


def rest_mask(n_chan, plan):
    mask = jnp.int32(0)
    for o in range(3, n_chan - 1):
        for r in range(ROUNDS):
            mask += (plan[r] == o).astype(jnp.int32) << (o - 3)
    return mask


def place_of(offset, plan):
    place = jnp.int32(ROUNDS)
    for r in range(ROUNDS):
        place = jnp.where(plan[r] == offset, r, place)
    return place


def spectra_kernel(flags_hbm, basis_hbm, sums_hbm, record_hbm, spec_ref, held, basis, sums_held, flags, sems):
    windows, samples, width = record_hbm.shape
    copies = [
        pltpu.make_async_copy(record_hbm.at[w], held.at[w, pl.ds(0, samples)], sems.at[w]) for w in range(windows)
    ]
    small = [(basis_hbm, basis), (flags_hbm, flags), (sums_hbm, sums_held)]
    small = [pltpu.make_async_copy(src, dst, sems.at[windows + i]) for i, (src, dst) in enumerate(small)]
    copies[0].start()
    for copy in small + copies[1:]:
        copy.start()
    pad = held.shape[1] - samples
    for w in range(windows):
        held[w, samples:, :] = jnp.zeros((pad, width), BF16)
    for copy in small:
        copy.wait()
    good = flags[...].astype(F32) * (1.0 / math.sqrt(samples))
    sums = jnp.concatenate([sums_held[...]] * (width // 128), axis=1)
    rows = 2 * NFREQ
    for w in range(windows):
        copies[w].wait()
        out = jnp.dot(basis[...], held[w], preferred_element_type=F32)
        mean = out[rows : rows + 1] * (1.0 / samples)
        centred = held[w, :samples, :].astype(F32) - mean
        power = jnp.sum(centred * centred, axis=0, keepdims=True) * (1.0 / samples)
        scale = good / jnp.sqrt(power + 1e-05)
        spec_ref[w * rows : (w + 1) * rows, :] = ((out[:rows] - sums * mean) * scale).astype(BF16)


def turn_kernel(n_chan, plan_ref, mine_ref, other_ref, table_ref, turned_ref, mask_ref):
    mask_ref[0] = rest_mask(n_chan, [plan_ref[r] for r in range(ROUNDS)]) if few_sets(n_chan) else jnp.int32(0)
    lags = turned_ref.shape[0]
    first = lax.axis_index("tm") * lags
    depth, width = mine_ref.shape
    for half, ref in enumerate((mine_ref, other_ref)):
        for lag in range(lags):
            cosine = jnp.concatenate([table_ref[first + lag, 0]] * (width // 128), axis=1)
            sine = jnp.concatenate([table_ref[first + lag, 1]] * (width // 128), axis=1)
            parts = []
            for w in range(depth // (2 * NFREQ)):
                start = w * 2 * NFREQ
                real = ref[start : start + NFREQ, :].astype(F32)
                imag = ref[start + NFREQ : start + 2 * NFREQ, :].astype(F32)
                parts += [real * cosine + imag * sine, imag * cosine - real * sine]
            turned = jnp.concatenate(parts, axis=0).T.astype(BF16)
            turned_ref[lag, :, half * depth : (half + 1) * depth] = turned


def correlate_kernel(scale, labels, plan_ref, turned_ref, *refs):
    blocks = len(labels)
    mine, other, (out_ref, held, sems) = refs[:blocks], refs[blocks : 2 * blocks], refs[-3:]
    lags, _, depth = turned_ref.shape
    half = depth // 2
    plan = [plan_ref[r] for r in range(ROUNDS)]
    places = []
    for s, label in enumerate(labels):
        if isinstance(label, tuple):
            label = jnp.where(lax.axis_index("tm") == 0, *label)
        places.append(jnp.int32(s) if label is None else place_of(label, plan))

    def copy(s, lag):
        return pltpu.make_async_copy(held.at[s, lag], out_ref.at[lag, places[s]], sems.at[s, lag])

    for s in range(blocks):

        @pl.when(places[s] < ROUNDS)
        def _():
            for lag in range(lags):
                total = jnp.dot(turned_ref[lag, :, :half], mine[s][...], preferred_element_type=F32)
                total += jnp.dot(turned_ref[lag, :, half:], other[s][...], preferred_element_type=F32)
                held[s, lag] = (total * scale).astype(BF16)
                copy(s, lag).start()

    for s in range(blocks):

        @pl.when(places[s] < ROUNDS)
        def _():
            for lag in range(lags):
                copy(s, lag).wait()


def correlate(plan, turned, pairs, labels, out=None):
    lags, width, depth = turned.shape
    blocks = len(pairs)
    scale = 1.0 / math.sqrt(depth // 2)
    given = [plan, turned] + [p[0] for p in pairs] + [p[1] for p in pairs]
    specs = [pl.BlockSpec(memory_space=SMEM)] + [pl.BlockSpec(memory_space=VMEM)] * (1 + 2 * blocks)
    if out is not None:
        given.append(out)
        specs.append(pl.BlockSpec(memory_space=HBM))
    return pl.pallas_call(
        partial(correlate_kernel, scale, labels),
        out_shape=HBM((lags, ROUNDS, width, width), BF16),
        in_specs=specs,
        out_specs=pl.BlockSpec(memory_space=HBM),
        scratch_shapes=[
            pltpu.VMEM((blocks, lags, width, width), BF16),
            pltpu.SemaphoreType.DMA((blocks, lags)),
        ],
        input_output_aliases={} if out is None else {len(given) - 1: 0},
        compiler_params=pltpu.CompilerParams(vmem_limit_bytes=KERNEL_VMEM),
        cost_estimate=pl.CostEstimate(flops=blocks << 28, bytes_accessed=blocks << 20, transcendentals=0),
        name="correlate",
    )(*given)


def turn(spec, samples, plan):
    depth, width = spec.shape
    other = swap(spec)
    return pl.pallas_call(
        partial(turn_kernel, lax.axis_size("chan")),
        out_shape=(
            jax.ShapeDtypeStruct((LAGS // 2, width, 2 * depth), BF16),
            jax.ShapeDtypeStruct((1,), jnp.int32),
        ),
        in_specs=[pl.BlockSpec(memory_space=SMEM)] + [pl.BlockSpec(memory_space=VMEM)] * 3,
        out_specs=(pl.BlockSpec(memory_space=VMEM), pl.BlockSpec(memory_space=SMEM)),
        compiler_params=pltpu.CompilerParams(vmem_limit_bytes=KERNEL_VMEM),
        cost_estimate=pl.CostEstimate(flops=4 << 20, bytes_accessed=4 << 20, transcendentals=0),
        name="turn",
    )(plan, spec, other, jnp.asarray(turn_table(samples)))


KERNEL_VMEM = 8 << 20


def few_sets(n_chan):
    return n_chan == 2 * ROUNDS


def hop(value, offset):
    pairs = [(source, source ^ offset) for source in range(lax.axis_size("chan"))]
    return lax.ppermute(value, "chan", pairs)


def swap(value):
    return lax.ppermute(value, "tm", [(0, 1), (1, 0)])


def with_swap(block):
    return block, swap(block)


def split_hop(first, second, hops):
    n_chan = lax.axis_size("chan")
    value = first if first is second else jnp.where(lax.axis_index("tm") == 0, first, second)
    pairs = [(2 * c + t, 2 * (c ^ hops[t]) + t) for c in range(n_chan) for t in range(2)]
    return lax.ppermute(value, ("chan", "tm"), pairs)


def correlate_rest(mask, crossed, near, turned, plan, out):
    top = lax.axis_size("chan") - 1
    here = {1: near[0], 2: near[1], top: crossed}
    wanted = [o + 3 for o in range(mask.bit_length()) if mask >> o & 1][: ROUNDS - 1]
    route = {o: (top, o ^ top) for o in wanted}
    if 3 in wanted:
        route[3] = (2, 1) if 5 in wanted or 4 in wanted else (1, 2)
    pairs, labels = [], list(wanted)
    if wanted == [3]:
        pairs = [with_swap(split_hop(here[1], here[2], (2, 1)))]
    elif len(wanted) == 2 and 4 not in wanted:
        (src0, hop0), (src1, hop1) = route[wanted[0]], route[wanted[1]]
        got0 = split_hop(here[src0], here[src1], (hop0, hop1))
        got1 = split_hop(here[src1], here[src0], (hop1, hop0))
        pairs = [(got0, swap(got1)), (got1, swap(got0))]
        labels = [tuple(wanted), tuple(wanted[::-1])]
    else:
        pairs = [with_swap(hop(here[src], by)) for src, by in (route[o] for o in wanted)]
    if not pairs:
        return correlate(plan, turned, [with_swap(crossed)], [top], out)
    out = correlate(plan, turned, [with_swap(crossed)], [top], out)
    return correlate(plan, turned, pairs, labels, out)


def fetch_by_bits(spec, plan):
    bits = lax.axis_size("chan").bit_length() - 1
    partners = [spec] * ROUNDS
    for bit in range(bits):
        moves = jnp.right_shift(plan, bit) & 1 == 1
        for r in range(ROUNDS):
            partners[r] = lax.cond(moves[r], partial(hop, offset=2**bit), lambda v: v, partners[r])
    return partners


def on_device(record, flags, plan):
    windows, width, samples = record.shape
    n_chan = lax.axis_size("chan")
    depth = windows * 2 * NFREQ
    basis, sums = basis_table(samples)
    spec = pl.pallas_call(
        spectra_kernel,
        out_shape=VMEM((depth, width), BF16),
        in_specs=[pl.BlockSpec(memory_space=pl.ANY)] * 4,
        out_specs=pl.BlockSpec(memory_space=VMEM),
        scratch_shapes=[
            pltpu.VMEM((windows, padded(samples), width), BF16),
            pltpu.VMEM(basis.shape, BF16),
            pltpu.VMEM(sums.shape, F32),
            pltpu.VMEM((1, width), jnp.int32),
            pltpu.SemaphoreType.DMA((windows + 3,)),
        ],
        compiler_params=pltpu.CompilerParams(vmem_limit_bytes=66_000_000),
        name="spectra",
    )(flags.reshape(1, width), jnp.asarray(basis), jnp.asarray(sums), record.transpose(0, 2, 1))

    if few_sets(n_chan):
        crossed = hop(spec, n_chan - 1)
        near = [hop(spec, 1), hop(spec, 2)]
        turned, mask = turn(spec, samples, plan)
        out = correlate(plan, turned, [with_swap(block) for block in near], [1, 2])
        branches = [partial(correlate_rest, m) for m in range(2 ** (n_chan - 4))]
        return lax.switch(mask[0], branches, crossed, near, turned, plan, out)
    pairs = [with_swap(m) for m in fetch_by_bits(spec, plan)]
    return correlate(plan, turn(spec, samples, plan)[0], pairs, [None] * ROUNDS)


def solution(mesh):
    def step(record, flags, plan):
        return on_device(record, flags, plan)

    step = jax.shard_map(
        step,
        mesh=mesh,
        in_specs=(P("tm", ("groups", "chan"), None), P(("groups", "chan")), P()),
        out_specs=P("tm", None, ("groups", "chan"), None),
        check_vma=False,
    )
    return step
```

```python
from functools import partial
import math

import numpy as np

import jax
import jax.numpy as jnp
from jax import lax
from jax.experimental import pallas as pl
from jax.experimental.pallas import tpu as pltpu
from jax.sharding import PartitionSpec as P


NFREQ = 32
FLO = 5
LAGS = 4
LAGSTEP = 3
ROUNDS = 4

TWO_PI = 2.0 * math.pi
VMEM = pltpu.MemorySpace.VMEM
SMEM = pltpu.MemorySpace.SMEM
HBM = pltpu.MemorySpace.HBM
BF16 = jnp.bfloat16
F32 = jnp.float32


def padded(samples):
    return -(-samples // 256) * 256


def basis_table(samples):
    phase = (FLO + np.arange(NFREQ))[:, None] * np.arange(samples)[None, :] % samples
    angle = phase.astype(np.float32) * np.float32(TWO_PI / samples)
    rows = np.concatenate([np.cos(angle), -np.sin(angle)], 0).astype(jnp.bfloat16)
    table = np.zeros((2 * NFREQ + 16, padded(samples)), jnp.bfloat16)
    table[: 2 * NFREQ, :samples] = rows
    table[2 * NFREQ, :samples] = 1
    sums = rows.astype(np.float64).sum(1).astype(np.float32)
    return table, np.repeat(sums[:, None], 128, 1)


def turn_table(samples):
    ticks = (np.arange(LAGS) - LAGS // 2) * LAGSTEP
    phase = (FLO + np.arange(NFREQ))[None, :] * ticks[:, None] % samples
    angle = phase.astype(np.float32) * np.float32(TWO_PI / samples)
    table = np.stack([np.cos(angle), np.sin(angle)], 1).astype(np.float32)
    return np.repeat(table[..., None], 128, 3)


def place_of(offset, plan):
    place = jnp.int32(ROUNDS)
    for r in range(ROUNDS):
        place = jnp.where(plan[r] == offset, r, place)
    return place


def spectra_kernel(flags_hbm, basis_hbm, sums_hbm, record_hbm, spec_ref, held, basis, sums_held, flags, sems):
    windows, samples, width = record_hbm.shape
    copies = [
        pltpu.make_async_copy(record_hbm.at[w], held.at[w, pl.ds(0, samples)], sems.at[w]) for w in range(windows)
    ]
    small = [(basis_hbm, basis), (flags_hbm, flags), (sums_hbm, sums_held)]
    small = [pltpu.make_async_copy(src, dst, sems.at[windows + i]) for i, (src, dst) in enumerate(small)]
    copies[0].start()
    for copy in small + copies[1:]:
        copy.start()
    pad = held.shape[1] - samples
    for w in range(windows):
        held[w, samples:, :] = jnp.zeros((pad, width), BF16)
    for copy in small:
        copy.wait()
    good = flags[...].astype(F32) * (1.0 / math.sqrt(samples))
    sums = jnp.concatenate([sums_held[...]] * (width // 128), axis=1)
    rows = 2 * NFREQ
    for w in range(windows):
        copies[w].wait()
        out = jnp.dot(basis[...], held[w], preferred_element_type=F32)
        mean = out[rows : rows + 1] * (1.0 / samples)
        centred = held[w, :samples, :].astype(F32) - mean
        power = jnp.sum(centred * centred, axis=0, keepdims=True) * (1.0 / samples)
        scale = good / jnp.sqrt(power + 1e-05)
        spec_ref[w * rows : (w + 1) * rows, :] = ((out[:rows] - sums * mean) * scale).astype(BF16)


def turn_kernel(mine_ref, other_ref, table_ref, turned_ref):
    lags = turned_ref.shape[0]
    first = lax.axis_index("tm") * lags
    depth, width = mine_ref.shape
    for half, ref in enumerate((mine_ref, other_ref)):
        for lag in range(lags):
            cosine = jnp.concatenate([table_ref[first + lag, 0]] * (width // 128), axis=1)
            sine = jnp.concatenate([table_ref[first + lag, 1]] * (width // 128), axis=1)
            parts = []
            for w in range(depth // (2 * NFREQ)):
                start = w * 2 * NFREQ
                real = ref[start : start + NFREQ, :].astype(F32)
                imag = ref[start + NFREQ : start + 2 * NFREQ, :].astype(F32)
                parts += [real * cosine + imag * sine, imag * cosine - real * sine]
            turned = jnp.concatenate(parts, axis=0).T.astype(BF16)
            turned_ref[lag, :, half * depth : (half + 1) * depth] = turned


def correlate_kernel(scale, labels, plan_ref, turned_ref, *refs):
    blocks = len(labels)
    mine, other, (out_ref, held, sems) = refs[:blocks], refs[blocks : 2 * blocks], refs[-3:]
    lags, _, depth = turned_ref.shape
    half = depth // 2
    plan = [plan_ref[r] for r in range(ROUNDS)]
    places = []
    for s, label in enumerate(labels):
        if isinstance(label, tuple):
            label = jnp.where(lax.axis_index("tm") == 0, *label)
        places.append(jnp.int32(s) if label is None else place_of(label, plan))

    def copy(s, lag):
        return pltpu.make_async_copy(held.at[s, lag], out_ref.at[lag, places[s]], sems.at[s, lag])

    for s in range(blocks):

        @pl.when(places[s] < ROUNDS)
        def _():
            for lag in range(lags):
                total = jnp.dot(turned_ref[lag, :, :half], mine[s][...], preferred_element_type=F32)
                total += jnp.dot(turned_ref[lag, :, half:], other[s][...], preferred_element_type=F32)
                held[s, lag] = (total * scale).astype(BF16)
                copy(s, lag).start()

    for s in range(blocks):

        @pl.when(places[s] < ROUNDS)
        def _():
            for lag in range(lags):
                copy(s, lag).wait()


def correlate(plan, turned, pairs, labels, out=None):
    lags, width, depth = turned.shape
    blocks = len(pairs)
    scale = 1.0 / math.sqrt(depth // 2)
    given = [plan, turned] + [p[0] for p in pairs] + [p[1] for p in pairs]
    specs = [pl.BlockSpec(memory_space=SMEM)] + [pl.BlockSpec(memory_space=VMEM)] * (1 + 2 * blocks)
    if out is not None:
        given.append(out)
        specs.append(pl.BlockSpec(memory_space=HBM))
    return pl.pallas_call(
        partial(correlate_kernel, scale, labels),
        out_shape=HBM((lags, ROUNDS, width, width), BF16),
        in_specs=specs,
        out_specs=pl.BlockSpec(memory_space=HBM),
        scratch_shapes=[
            pltpu.VMEM((blocks, lags, width, width), BF16),
            pltpu.SemaphoreType.DMA((blocks, lags)),
        ],
        input_output_aliases={} if out is None else {len(given) - 1: 0},
        compiler_params=pltpu.CompilerParams(vmem_limit_bytes=KERNEL_VMEM),
        cost_estimate=pl.CostEstimate(flops=blocks << 28, bytes_accessed=blocks << 20, transcendentals=0),
        name="correlate",
    )(*given)


def turn(spec, other, samples):
    depth, width = spec.shape
    return pl.pallas_call(
        turn_kernel,
        out_shape=VMEM((LAGS // 2, width, 2 * depth), BF16),
        in_specs=[pl.BlockSpec(memory_space=VMEM)] * 3,
        out_specs=pl.BlockSpec(memory_space=VMEM),
        compiler_params=pltpu.CompilerParams(vmem_limit_bytes=KERNEL_VMEM),
        cost_estimate=pl.CostEstimate(flops=4 << 20, bytes_accessed=4 << 20, transcendentals=0),
        name="turn",
    )(spec, other, jnp.asarray(turn_table(samples)))


KERNEL_VMEM = 8 << 20


def few_sets(n_chan):
    return n_chan == 2 * ROUNDS


def hop(value, offset):
    pairs = [(source, source ^ offset) for source in range(lax.axis_size("chan"))]
    return lax.ppermute(value, "chan", pairs)


def swap(value):
    return lax.ppermute(value, "tm", [(0, 1), (1, 0)])


def with_swap(block):
    return block, swap(block)


def fetch_by_bits(spec, plan):
    bits = lax.axis_size("chan").bit_length() - 1
    partners = [spec] * ROUNDS
    for bit in range(bits):
        moves = jnp.right_shift(plan, bit) & 1 == 1
        for r in range(ROUNDS):
            partners[r] = lax.cond(moves[r], partial(hop, offset=2**bit), lambda v: v, partners[r])
    return partners


def on_device(record, flags, plan):
    windows, width, samples = record.shape
    n_chan = lax.axis_size("chan")
    depth = windows * 2 * NFREQ
    basis, sums = basis_table(samples)
    spec = pl.pallas_call(
        spectra_kernel,
        out_shape=VMEM((depth, width), BF16),
        in_specs=[pl.BlockSpec(memory_space=pl.ANY)] * 4,
        out_specs=pl.BlockSpec(memory_space=VMEM),
        scratch_shapes=[
            pltpu.VMEM((windows, padded(samples), width), BF16),
            pltpu.VMEM(basis.shape, BF16),
            pltpu.VMEM(sums.shape, F32),
            pltpu.VMEM((1, width), jnp.int32),
            pltpu.SemaphoreType.DMA((windows + 3,)),
        ],
        compiler_params=pltpu.CompilerParams(vmem_limit_bytes=66_000_000),
        name="spectra",
    )(flags.reshape(1, width), jnp.asarray(basis), jnp.asarray(sums), record.transpose(0, 2, 1))

    if not few_sets(n_chan):
        pairs = [with_swap(m) for m in fetch_by_bits(spec, plan)]
        return correlate(plan, turn(spec, swap(spec), samples), pairs, [None] * ROUNDS)

    got = {0: spec}
    for offset, source in HOPS:
        got[offset] = hop(got[source], offset ^ source)
    pairs = {}
    for offset in got:
        pairs[offset] = with_swap(got[offset])
    turned = turn(*pairs[0], samples)
    out = None
    for group in GROUPS:
        out = correlate(plan, turned, [pairs[o] for o in group], group, out)
    return out


HOPS = ((7, 0), (2, 0), (1, 0), (6, 0), (5, 7), (4, 2), (3, 2))
GROUPS = ((7, 2, 1, 6), (5, 4, 3))


def solution(mesh):
    def step(record, flags, plan):
        return on_device(record, flags, plan)

    step = jax.shard_map(
        step,
        mesh=mesh,
        in_specs=(P("tm", ("groups", "chan"), None), P(("groups", "chan")), P()),
        out_specs=P("tm", None, ("groups", "chan"), None),
        check_vma=False,
    )
    return step
```

```python
from functools import partial
import itertools
import math

import numpy as np

import jax
import jax.numpy as jnp
from jax import lax
from jax.experimental import pallas as pl
from jax.experimental.pallas import tpu as pltpu
from jax.sharding import PartitionSpec as P


NFREQ = 32
FLO = 5
LAGS = 4
LAGSTEP = 3
ROUNDS = 4

TWO_PI = 2.0 * math.pi
VMEM = pltpu.MemorySpace.VMEM
SMEM = pltpu.MemorySpace.SMEM
HBM = pltpu.MemorySpace.HBM
BF16 = jnp.bfloat16
F32 = jnp.float32


def padded(samples):
    return -(-samples // 256) * 256


def basis_table(samples):
    phase = (FLO + np.arange(NFREQ))[:, None] * np.arange(samples)[None, :] % samples
    angle = phase.astype(np.float32) * np.float32(TWO_PI / samples)
    rows = np.concatenate([np.cos(angle), -np.sin(angle)], 0).astype(jnp.bfloat16)
    table = np.zeros((2 * NFREQ + 16, padded(samples)), jnp.bfloat16)
    table[: 2 * NFREQ, :samples] = rows
    table[2 * NFREQ, :samples] = 1
    sums = rows.astype(np.float64).sum(1).astype(np.float32)
    return table, np.repeat(sums[:, None], 128, 1)


def turn_table(samples):
    ticks = (np.arange(LAGS) - LAGS // 2) * LAGSTEP
    phase = (FLO + np.arange(NFREQ))[None, :] * ticks[:, None] % samples
    angle = phase.astype(np.float32) * np.float32(TWO_PI / samples)
    table = np.stack([np.cos(angle), np.sin(angle)], 1).astype(np.float32)
    return np.repeat(table[..., None], 128, 3)


def offset_sets(n_chan):
    return sorted(itertools.combinations(range(1, n_chan - 1), ROUNDS - 1), key=lambda s: s[::-1])


def set_index(plan):
    index = jnp.int32(0)
    for r in range(ROUNDS):
        rank = sum((plan[j] < plan[r]).astype(jnp.int32) for j in range(ROUNDS) if j != r)
        below = plan[r] - 1
        pairs = below * (below - 1) // 2
        triples = below * (below - 1) * (below - 2) // 6
        term = jnp.where(rank == 0, below, jnp.where(rank == 1, pairs, triples))
        index += jnp.where(rank == ROUNDS - 1, 0, term)
    return index


def place_of(offset, plan):
    place = jnp.int32(0)
    for r in range(ROUNDS):
        place = jnp.where(plan[r] == offset, r, place)
    return place


def spectra_kernel(
    n_chan, plan_ref, flags_hbm, basis_hbm, sums_hbm, record_hbm, spec_ref, index_ref, held, basis, sums_held, flags, sems
):
    windows, samples, width = record_hbm.shape
    copies = [
        pltpu.make_async_copy(record_hbm.at[w], held.at[w, pl.ds(0, samples)], sems.at[w]) for w in range(windows)
    ]
    small = [(basis_hbm, basis), (flags_hbm, flags), (sums_hbm, sums_held)]
    small = [pltpu.make_async_copy(src, dst, sems.at[windows + i]) for i, (src, dst) in enumerate(small)]
    copies[0].start()
    for copy in small + copies[1:]:
        copy.start()
    index_ref[0] = set_index([plan_ref[r] for r in range(ROUNDS)]) if few_sets(n_chan) else jnp.int32(0)
    pad = held.shape[1] - samples
    for w in range(windows):
        held[w, samples:, :] = jnp.zeros((pad, width), BF16)
    for copy in small:
        copy.wait()
    good = flags[...].astype(F32) * (1.0 / math.sqrt(samples))
    sums = jnp.concatenate([sums_held[...]] * (width // 128), axis=1)
    rows = 2 * NFREQ
    for w in range(windows):
        copies[w].wait()
        out = jnp.dot(basis[...], held[w], preferred_element_type=F32)
        mean = out[rows : rows + 1] * (1.0 / samples)
        centred = held[w, :samples, :].astype(F32) - mean
        power = jnp.sum(centred * centred, axis=0, keepdims=True) * (1.0 / samples)
        scale = good / jnp.sqrt(power + 1e-05)
        spec_ref[w * rows : (w + 1) * rows, :] = ((out[:rows] - sums * mean) * scale).astype(BF16)


def turn_kernel(mine_ref, other_ref, table_ref, turned_ref):
    lags = turned_ref.shape[0]
    first = lax.axis_index("tm") * lags
    depth, width = mine_ref.shape

    @pl.loop(0, lags)
    def _(lag):
        cosine = jnp.concatenate([table_ref[first + lag, 0]] * (width // 128), axis=1)
        sine = jnp.concatenate([table_ref[first + lag, 1]] * (width // 128), axis=1)
        for half, ref in enumerate((mine_ref, other_ref)):
            parts = []
            for w in range(depth // (2 * NFREQ)):
                start = w * 2 * NFREQ
                real = ref[start : start + NFREQ, :].astype(F32)
                imag = ref[start + NFREQ : start + 2 * NFREQ, :].astype(F32)
                parts += [real * cosine + imag * sine, imag * cosine - real * sine]
            turned = jnp.concatenate(parts, axis=0).T.astype(BF16)
            turned_ref[lag, :, half * depth : (half + 1) * depth] = turned


def correlate_kernel(scale, labels, plan_ref, turned_ref, *refs):
    blocks = len(labels)
    mine, other, (out_ref, held, sems) = refs[:blocks], refs[blocks : 2 * blocks], refs[-3:]
    lags, _, depth = turned_ref.shape
    half = depth // 2
    plan = [plan_ref[r] for r in range(ROUNDS)]
    places = []
    for s, label in enumerate(labels):
        if isinstance(label, tuple):
            label = jnp.where(lax.axis_index("tm") == 0, *label)
        places.append(s if label is None else place_of(label, plan))

    def copy(s, lag):
        return pltpu.make_async_copy(held.at[s, lag], out_ref.at[lag, places[s]], sems.at[s, lag])

    @pl.loop(0, lags)
    def _(lag):
        for s in range(blocks):
            total = jnp.dot(turned_ref[lag, :, :half], mine[s][...], preferred_element_type=F32)
            total += jnp.dot(turned_ref[lag, :, half:], other[s][...], preferred_element_type=F32)
            held[s, lag] = (total * scale).astype(BF16)
            copy(s, lag).start()

    for s in range(blocks):
        for lag in range(lags):
            copy(s, lag).wait()


def correlate(plan, turned, pairs, labels, out=None):
    lags, width, depth = turned.shape
    blocks = len(pairs)
    scale = 1.0 / math.sqrt(depth // 2)
    given = [plan, turned] + [p[0] for p in pairs] + [p[1] for p in pairs]
    specs = [pl.BlockSpec(memory_space=SMEM)] + [pl.BlockSpec(memory_space=VMEM)] * (1 + 2 * blocks)
    if out is not None:
        given.append(out)
        specs.append(pl.BlockSpec(memory_space=HBM))
    return pl.pallas_call(
        partial(correlate_kernel, scale, labels),
        out_shape=HBM((lags, ROUNDS, width, width), BF16),
        in_specs=specs,
        out_specs=pl.BlockSpec(memory_space=HBM),
        scratch_shapes=[
            pltpu.VMEM((blocks, lags, width, width), BF16),
            pltpu.SemaphoreType.DMA((blocks, lags)),
        ],
        input_output_aliases={} if out is None else {len(given) - 1: 0},
        compiler_params=pltpu.CompilerParams(vmem_limit_bytes=KERNEL_VMEM),
        cost_estimate=pl.CostEstimate(flops=blocks << 28, bytes_accessed=blocks << 20, transcendentals=0),
        name="correlate",
    )(*given)


def turn(spec, other, table):
    depth, width = spec.shape
    return pl.pallas_call(
        turn_kernel,
        out_shape=VMEM((LAGS // 2, width, 2 * depth), BF16),
        in_specs=[pl.BlockSpec(memory_space=VMEM)] * 3,
        out_specs=pl.BlockSpec(memory_space=VMEM),
        compiler_params=pltpu.CompilerParams(vmem_limit_bytes=KERNEL_VMEM),
        cost_estimate=pl.CostEstimate(flops=4 << 20, bytes_accessed=4 << 20, transcendentals=0),
        name="turn",
    )(spec, other, table)


KERNEL_VMEM = 8 << 20


def few_sets(n_chan):
    return n_chan == 2 * ROUNDS


def hop(value, offset):
    pairs = [(source, source ^ offset) for source in range(lax.axis_size("chan"))]
    return lax.ppermute(value, "chan", pairs)


def swap(value):
    return lax.ppermute(value, "tm", [(0, 1), (1, 0)])


def with_swap(block):
    return block, swap(block)


def fetch_by_bits(spec, plan):
    bits = lax.axis_size("chan").bit_length() - 1
    partners = [spec] * ROUNDS
    for bit in range(bits):
        moves = jnp.right_shift(plan, bit) & 1 == 1
        for r in range(ROUNDS):
            partners[r] = lax.cond(moves[r], partial(hop, offset=2**bit), lambda v: v, partners[r])
    return partners


def on_device(record, flags, plan):
    windows, width, samples = record.shape
    n_chan = lax.axis_size("chan")
    depth = windows * 2 * NFREQ
    basis, sums = basis_table(samples)
    spec, index = pl.pallas_call(
        partial(spectra_kernel, n_chan),
        out_shape=(VMEM((depth, width), BF16), jax.ShapeDtypeStruct((1,), jnp.int32)),
        in_specs=[pl.BlockSpec(memory_space=SMEM)] + [pl.BlockSpec(memory_space=pl.ANY)] * 4,
        out_specs=(pl.BlockSpec(memory_space=VMEM), pl.BlockSpec(memory_space=SMEM)),
        scratch_shapes=[
            pltpu.VMEM((windows, padded(samples), width), BF16),
            pltpu.VMEM(basis.shape, BF16),
            pltpu.VMEM(sums.shape, F32),
            pltpu.VMEM((1, width), jnp.int32),
            pltpu.SemaphoreType.DMA((windows + 3,)),
        ],
        compiler_params=pltpu.CompilerParams(vmem_limit_bytes=66_000_000),
        name="spectra",
    )(plan, flags.reshape(1, width), jnp.asarray(basis), jnp.asarray(sums), record.transpose(0, 2, 1))

    table = lax.optimization_barrier(jnp.asarray(turn_table(samples)))
    if not few_sets(n_chan):
        pairs = [with_swap(m) for m in fetch_by_bits(spec, plan)]
        return correlate(plan, turn(spec, swap(spec), table), pairs, [None] * ROUNDS)
    branches = [partial(correlate_set, route_of(o)) for o in offset_sets(n_chan)]
    return lax.switch(index[0], branches, spec, plan, table)


def route_of(offsets):
    wanted = sorted(offsets) + [7]
    far = [o for o in wanted if o >= 4]
    near = [o for o in wanted if o < 4]
    cross = max(far, key=lambda c: (sum(o ^ c in (1, 2) for o in far), -c))
    first, later = [cross], [(o, cross) for o in far if o ^ cross == 3]
    beside = [o for o in far if o ^ cross in (1, 2)]
    later += [(tuple(beside), cross)] if len(beside) == 2 else [(o, cross) for o in beside]
    if near == [1, 2, 3]:
        near, later = [1, 2], later + [(3, 2)]
    return first + near, later


def split_hops(value, hops):
    n_chan = lax.axis_size("chan")
    pairs = [(2 * c + t, 2 * (c ^ hops[t]) + t) for c in range(n_chan) for t in range(2)]
    return lax.ppermute(value, ("chan", "tm"), pairs)


def correlate_set(route, spec, plan, table):
    first, later = route
    got = {0: spec}

    def swapped(offset):
        return swap(got[offset])

    for offset in first:
        got[offset] = hop(spec, offset)
    last, labels = [], []
    for offset, source in later:
        if isinstance(offset, tuple):
            low, high = offset
            for a, b in ((low, high), (high, low)):
                got[a] = split_hops(got[source], (a ^ source, b ^ source))
            last += [(got[low], swapped(high)), (got[high], swapped(low))]
            labels += [(low, high), (high, low)]
        else:
            got[offset] = hop(got[source], offset ^ source)
            last.append((got[offset], swapped(offset)))
            labels.append(offset)
    turned = turn(spec, swapped(0), table)
    out = correlate(plan, turned, [(got[o], swapped(o)) for o in first], first)
    return correlate(plan, turned, last, labels, out)


def solution(mesh):
    return jax.shard_map(
        on_device,
        mesh=mesh,
        in_specs=(P("tm", ("groups", "chan"), None), P(("groups", "chan")), P()),
        out_specs=P("tm", None, ("groups", "chan"), None),
        check_vma=False,
    )
```
